32 devices in a mesh: group: 8 (over y, x, core), tensor: 4 (over z).
Axes of the slice: x: 2, y: 2, z: 4, core: 2. Of those that a mesh axis runs over, the one named last changes fastest.
Arguments:
- hidden: bfloat16 [8, 2, 256, 4096], P('group', None, 'tensor'), may hold values from -6 to 6
- norm_gain: bfloat16 [4096], replicated, may hold values from 0.5 to 1.5
- w_query: bfloat16 [4096, 4096], P(None, 'tensor'), may hold values from -0.09375 to 0.09375
- w_key: bfloat16 [4096, 1024], P(None, 'tensor'), may hold values from -0.09375 to 0.09375
- w_value: bfloat16 [4096, 1024], P(None, 'tensor'), may hold values from -0.09375 to 0.09375
- w_output: bfloat16 [4096, 4096], P('tensor'), may hold values from -0.09375 to 0.09375
- prefix_pool: bfloat16 [16384, 8, 2048], P('group', None, 'tensor'), may hold values from -120 to 120
- page_table: int32 [8, 2, 1024], P('group'), may hold values from 0 to 1023, each once within a row
- prefix_len: int32 [8, 2], replicated, may hold values from 1024 to 8192
- source: int32 [8], replicated, may hold values from 0 to 7, as said below
- decode_owner: int32 [8, 32], replicated, may hold values from 0 to 7, as said below
Outputs:
- layer_out: bfloat16 [2048, 4096], P(('group', 'tensor'))
- decode_pool: bfloat16 [256, 8, 2048], P('group', None, 'tensor')
The draws below stay inside these ranges and needn't reach their ends.
Inputs may be any that keep to these rules, and one draw needn't show every extreme that they name: source[h] is h or h - 1 modulo 8. For each page index k, the values decode_owner[h, k] over all h are all different; no row names one group more than 4 times, and some row names a group exactly 4 times.
All inputs are finite; a program needn't handle non-finite values.
Results may differ from the reference program's by a relative error of at most 0.012.
Values may be sent and summed in bfloat16 or wider, within the bound.
A program may use at most 192 MiB of HBM per device.

```python
import math
import jax
import jax.numpy as jnp
from jax import lax

D = 4096
HQ = 32
KVH = 8
HD = 128
PAGE = 8
BLOCK = 256
PREFIX = 8192
GROUPS = 8
NPAGE = 32
PREF_PAGES = 1024
KV_COLS = 2048
N_TENSOR = 4


def draw_prefix_pool(key, part):
    values = jax.random.normal(key, (GROUPS * 2 * PREF_PAGES, PAGE, KV_COLS), jnp.float32)
    values = jnp.clip(values, -5.0, 5.0)
    return values.astype(jnp.bfloat16)


def draw_source(key, part):
    indices = jnp.arange(GROUPS)
    coins = jax.random.randint(jax.random.fold_in(key, 2), (GROUPS,), 0, 2)
    middle = GROUPS // 2
    forced = (indices == 0) | (indices == middle)
    takes = jnp.logical_or(forced, coins == 1)
    picked = jnp.where(takes, indices - 1, indices)
    return (picked % GROUPS).astype(jnp.int32)


def draw_decode_owner(key, part):
    spread_count = min(GROUPS, NPAGE - NPAGE // 4)
    offsets_all = jax.random.permutation(jax.random.fold_in(key, 1), GROUPS)
    relabel = jax.random.permutation(jax.random.fold_in(key, 2), GROUPS)
    offsets = offsets_all[jnp.arange(NPAGE) % spread_count]
    indices = jnp.arange(GROUPS)
    return relabel[(indices[:, None] + offsets[None, :]) % GROUPS].astype(jnp.int32)


def touch_ends(result, rng, low, high):
    shape = result.shape
    place = [jax.random.randint(jax.random.fold_in(rng, axis), (), 0, shape[axis]) for axis in range(len(shape))]
    result = result.at[tuple(place)].set(low)
    longest = shape.index(max(shape))
    place[longest] = (place[longest] + 1) % shape[longest]
    return result.at[tuple(place)].set(high)


def block_levels(rng, dims, pieces, least, top_value):
    def one(position, shards_of):
        heights = jax.random.uniform(jax.random.fold_in(jax.random.fold_in(rng, 6), position), (shards_of,), jnp.float32, least / len(pieces), top_value / len(pieces))
        return jnp.repeat(jnp.exp(heights), dims[position] // shards_of).reshape((-1,) + (1,) * (len(dims) - position - 1))

    factor_of = one(*pieces[0])
    for cut in pieces[1:]:
        factor_of = factor_of * one(*cut)
    return factor_of


def scatter_about(key, extent, width, most, pieces=(), held_as=jnp.bfloat16):
    drawn = jax.random.normal(key, extent, jnp.float32) * width
    if len(pieces) > 0:
        drawn = block_levels(key, extent, pieces, -0.22, 0.18) * drawn
    return jnp.clip(drawn, min=-most, max=most).astype(held_as)


def setup_inputs(seed: int = 0) -> dict:
    arg_keys = jax.random.split(jax.random.key(seed), 12)
    hidden = scatter_about(arg_keys[0], (GROUPS, 2, BLOCK, D), 1.0, 6.0, ((0, 8), (2, 4)))
    norm_gain = jnp.clip(1.0 + 0.1 * jax.random.normal(arg_keys[1], (D,), jnp.float32), 0.5, 1.5).astype(jnp.bfloat16)
    w_query = scatter_about(arg_keys[2], (D, HQ * HD), D ** -0.5, 0.09375, ((1, 4),))
    w_key = scatter_about(arg_keys[3], (D, KVH * HD), D ** -0.5, 0.09375, ((1, 4),))
    w_value = scatter_about(arg_keys[4], (D, KVH * HD), D ** -0.5, 0.09375, ((1, 4),))
    w_output = scatter_about(arg_keys[5], (HQ * HD, D), (HQ * HD) ** -0.5, 0.09375, ((0, 4),))
    prefix_pool = draw_prefix_pool(jax.random.fold_in(arg_keys[11], 71), 0)
    page_table = jax.vmap(lambda own: jax.random.permutation(own, PREF_PAGES))(jax.random.split(arg_keys[7], GROUPS * 2)).reshape((GROUPS, 2, PREF_PAGES)).astype(jnp.int32)
    prefix_len = touch_ends(jax.random.randint(arg_keys[8], (GROUPS, 2), PREFIX // 8, PREFIX + 1), jax.random.fold_in(arg_keys[8], 1), PREFIX // 8, PREFIX).astype(jnp.int32)
    source = draw_source(jax.random.fold_in(arg_keys[11], 71), 0)
    decode_owner = draw_decode_owner(jax.random.fold_in(arg_keys[11], 71), 0)
    return {"hidden": hidden, "norm_gain": norm_gain, "w_query": w_query, "w_key": w_key, "w_value": w_value, "w_output": w_output, "prefix_pool": prefix_pool, "page_table": page_table, "prefix_len": prefix_len, "source": source, "decode_owner": decode_owner}


EPS = 1e-05
THETA = 500000.0

def rotate(values, positions):
    half_dim = values.shape[-1] // 2
    frequency = THETA ** (-(jnp.arange(half_dim, dtype=jnp.float32) * 2.0) / values.shape[-1])
    angles = positions[..., None] * frequency
    cosine = jnp.cos(angles)[..., None, :]
    sines = jnp.sin(angles)[..., None, :]
    first_half = values[..., :half_dim]
    second = values[..., half_dim:]
    return jnp.concatenate([first_half * cosine - second * sines, second * cosine + first_half * sines], axis=-1)

def reference(hidden, norm_gain, w_query, w_key, w_value, w_output, prefix_pool, page_table, prefix_len, source, decode_owner):
    group_size = HQ // KVH
    score_scale = 1.0 / math.sqrt(HD)
    flat_hidden = hidden.reshape(GROUPS * 2, BLOCK, D)
    flat_table = page_table.reshape(GROUPS * 2, PREF_PAGES)
    flat_len = prefix_len.reshape(GROUPS * 2)

    def one_group(slot_index):
        owner_group = source[slot_index].astype(jnp.int32)
        slot = jnp.where(owner_group == slot_index, 0, 1).astype(jnp.int32)
        entry = (owner_group * 2 + slot).astype(jnp.int32)
        prefix_count = flat_len[entry]
        block_rows = lax.dynamic_slice_in_dim(flat_hidden, entry, 1, 0)[0]
        block_f32 = block_rows.astype(jnp.float32)
        mean_square = lax.optimization_barrier(jnp.mean(block_f32 * block_f32, axis=-1, keepdims=True))
        normed = (block_f32 * lax.rsqrt(mean_square + EPS) * norm_gain.astype(jnp.float32)).astype(jnp.bfloat16)
        queries = jnp.dot(normed, w_query, preferred_element_type=jnp.float32).reshape(BLOCK, HQ, HD)
        new_keys = jnp.dot(normed, w_key, preferred_element_type=jnp.float32).reshape(BLOCK, KVH, HD)
        new_values = jnp.dot(normed, w_value, preferred_element_type=jnp.float32).reshape(BLOCK, KVH, HD).astype(jnp.bfloat16)
        positions = (prefix_count + jnp.arange(BLOCK, dtype=jnp.int32)).astype(jnp.float32)
        queries = rotate(queries, positions).astype(jnp.bfloat16)
        new_keys = rotate(new_keys, positions).astype(jnp.bfloat16)
        slot_order = lax.dynamic_slice_in_dim(flat_table, entry, 1, 0)[0].astype(jnp.int32)
        prefix_kv = jnp.take(prefix_pool, entry * PREF_PAGES + slot_order, axis=0)
        prefix_kv = prefix_kv.reshape(PREFIX, KVH, 2, HD)
        all_keys = jnp.concatenate([prefix_kv[:, :, 0], new_keys], axis=0)
        values = jnp.concatenate([prefix_kv[:, :, 1], new_values], axis=0)
        column = jnp.arange(PREFIX + BLOCK, dtype=jnp.int32)[None, :]
        row_index = jnp.arange(BLOCK, dtype=jnp.int32)[:, None]
        allowed = jnp.where(column < PREFIX, column < prefix_count, column - PREFIX <= row_index)
        grouped = queries.reshape(BLOCK, KVH, group_size, HD).astype(jnp.float32)
        scores = jnp.einsum('qhgd,khd->hgqk', grouped, all_keys.astype(jnp.float32)) * score_scale
        scores = jnp.where(allowed, scores, -jnp.inf)
        row_max = lax.optimization_barrier(jnp.max(scores, axis=-1, keepdims=True))
        exp_scores = jnp.where(allowed, jnp.exp(scores - row_max), 0.0)
        row_total = lax.optimization_barrier(jnp.sum(exp_scores, axis=-1))
        weights = exp_scores.astype(jnp.bfloat16)
        mixed_heads = jnp.einsum('hgqk,khd->qhgd', weights.astype(jnp.float32), values.astype(jnp.float32))
        attended = (mixed_heads / jnp.transpose(row_total, (2, 0, 1))[..., None]).astype(jnp.bfloat16)
        blocks = attended.reshape(BLOCK, N_TENSOR, HQ * HD // N_TENSOR).astype(jnp.float32)
        projections = w_output.reshape(N_TENSOR, HQ * HD // N_TENSOR, D).astype(jnp.float32)
        partial_value = jnp.einsum('qtc,tcd->tqd', blocks, projections).astype(jnp.bfloat16)
        summed = lax.optimization_barrier(jnp.sum(partial_value.astype(jnp.float32), axis=0))
        out_rows = (block_f32 + summed).astype(jnp.bfloat16)
        new_kv = jnp.stack([new_keys, new_values], axis=2).reshape(BLOCK, KV_COLS)
        return (out_rows, new_kv)
    block_outs, block_kv = lax.map(one_group, jnp.arange(GROUPS, dtype=jnp.int32))
    layer_out = block_outs.reshape(GROUPS * BLOCK, D)
    page_rows = block_kv.reshape(GROUPS * NPAGE, PAGE, KV_COLS)
    pool_slots = (decode_owner.astype(jnp.int32) * NPAGE + jnp.arange(NPAGE, dtype=jnp.int32)[None, :]).reshape(-1)
    kv_pool = jnp.zeros((GROUPS * NPAGE, PAGE, KV_COLS), jnp.bfloat16).at[pool_slots].set(page_rows)
    return (layer_out, kv_pool)
```

```python
import functools
import math

import numpy as np

import jax
import jax.numpy as jnp
from jax import lax
from jax.experimental import pallas as pl
from jax.experimental.pallas import tpu as pltpu
from jax.sharding import PartitionSpec as P

HD = 128
PAGE = 8
PAGE_BITS = 3
EPS = 1e-05
THETA = 500000.0
CHUNK = 1024
EXP_SCALE = math.log2(math.e) / math.sqrt(HD)
MESH = pl.DeviceIdType.MESH
VMEM = pl.BlockSpec(memory_space=pltpu.VMEM)
SMEM = pl.BlockSpec(memory_space=pltpu.SMEM)
ANY = pl.BlockSpec(memory_space=pl.ANY)


def greet(barrier, peers, me, size):
    for peer in peers:
        pl.semaphore_signal(barrier, inc=1, device_id={"group": peer}, device_id_type=MESH)
    for target in (me + 1, me - 1):

        @pl.when(jnp.logical_and(target >= 0, target < size))
        def _():
            pl.semaphore_signal(
                barrier,
                inc=1,
                device_id={"tensor": jnp.clip(target, 0, size - 1)},
                device_id_type=MESH,
            )

    near = jnp.where(me > 0, 1, 0) + jnp.where(me < size - 1, 1, 0)
    pl.semaphore_wait(barrier, near + len(peers))


def gather_kernel(
    source_ref,
    len_ref,
    freq_ref,
    gain_ref,
    hidden_hbm,
    wq_hbm,
    wk_hbm,
    wv_hbm,
    rows_ref,
    q_ref,
    new_ref,
    own,
    handed,
    flat,
    wq,
    wk,
    wv,
    cosines,
    sines,
    turned,
    own_sem,
    w_sems,
    hand_sems,
    send,
    recv,
    lend_sems,
):
    group, groups = lax.axis_index("group"), lax.axis_size("group")
    me, size = lax.axis_index("tensor"), lax.axis_size("tensor")
    upper, lower = (group + 1) % groups, (group + groups - 1) % groups
    count, width = own.shape
    piece = hand_count(count)
    pieces = count // piece
    tiles, _, wide = wq.shape
    kv_heads = wk.shape[1] // HD
    heads = tiles * wide // HD // kv_heads
    columns = q_ref.shape[4]

    own_copy = pltpu.make_async_copy(hidden_hbm.at[0], own, own_sem)
    own_copy.start()
    fetches = []
    for i in range(tiles):
        fetches.append(
            pltpu.make_async_copy(wq_hbm.at[:, pl.ds(i * wide, wide)], wq.at[i], w_sems.at[i])
        )
    fetches.append(pltpu.make_async_copy(wk_hbm, wk, w_sems.at[tiles]))
    fetches.append(pltpu.make_async_copy(wv_hbm, wv, w_sems.at[tiles + 1]))
    greet(pltpu.get_barrier_semaphore(), (upper, lower), me, size)

    def hand(p):
        return pltpu.make_async_remote_copy(
            src_ref=hidden_hbm.at[1, pl.ds(p * piece, piece)],
            dst_ref=handed.at[pl.ds(p * piece, piece)],
            send_sem=hand_sems.at[0, p],
            recv_sem=hand_sems.at[1, p],
            device_id={"group": upper},
            device_id_type=MESH,
        )

    for p in range(pieces):
        hand(p).start()
    for fetch in fetches:
        fetch.start()

    def part(direction, step, p):
        start = (me - direction * step) * count + p * piece
        ref = flat.at[pl.ds(pl.multiple_of(start, piece), piece)]
        lane = 0 if direction > 0 else 1
        return pltpu.make_async_remote_copy(
            src_ref=ref,
            dst_ref=ref,
            send_sem=send.at[lane, step, p],
            recv_sem=recv.at[lane, step, p],
            device_id={"tensor": jnp.clip(me + direction, 0, size - 1)},
            device_id_type=MESH,
        )

    def landed(direction, step, p):
        start = (me - direction * step) * count + p * piece
        ref = flat.at[pl.ds(pl.multiple_of(start, piece), piece)]
        lane = 0 if direction > 0 else 1
        return pltpu.make_async_remote_copy(
            src_ref=ref,
            dst_ref=ref,
            send_sem=send.at[lane, step - 1, p],
            recv_sem=recv.at[lane, step - 1, p],
            device_id={"tensor": jnp.clip(me + direction, 0, size - 1)},
            device_id_type=MESH,
        )

    def holds(direction, step):
        start = me - direction * step
        return jnp.logical_and(start >= 0, start < size)

    def sends(direction, step):
        target = me + direction
        return jnp.logical_and(
            holds(direction, step), jnp.logical_and(target >= 0, target < size)
        )

    own_copy.wait()
    take = source_ref[group] != group
    gain = gain_ref[...].astype(jnp.float32)
    for p in range(pieces):
        hand(p).wait_recv()
        span = pl.ds(p * piece, piece)
        rows = jnp.where(take, handed[span, :].astype(jnp.float32), own[span, :].astype(jnp.float32))
        rows_ref[span, :] = rows.astype(rows_ref.dtype)
        mean_square = jnp.mean(rows * rows, axis=-1, keepdims=True)
        flat[pl.ds(pl.multiple_of(me * count + p * piece, piece), piece), :] = (
            rows * lax.rsqrt(mean_square + EPS) * gain
        ).astype(flat.dtype)
        for direction in (1, -1):

            @pl.when(sends(direction, 0))
            def _(direction=direction, p=p):
                part(direction, 0, p).start()

    prefix = jnp.where(take, len_ref[lower, 1], len_ref[group, 0])
    total = flat.shape[0]
    where_at = (lax.broadcasted_iota(jnp.int32, (total, HD), 0) + prefix).astype(jnp.float32)
    angles = where_at * freq_ref[...]
    cosines[...] = jnp.cos(angles)
    sines[...] = jnp.where(
        lax.broadcasted_iota(jnp.int32, (total, HD), 1) < HD // 2, -jnp.sin(angles), jnp.sin(angles)
    )

    for step in range(1, size):
        for p in range(pieces):
            for direction in (1, -1):

                @pl.when(holds(direction, step))
                def _(direction=direction, step=step, p=p):
                    landed(direction, step, p).wait_recv()

                if step < size - 1:

                    @pl.when(sends(direction, step))
                    def _(direction=direction, step=step, p=p):
                        part(direction, step, p).start()

    def rotate(values):
        return values * cosines[...] + pltpu.roll(values, HD // 2, 1) * sines[...]

    def lend(b, g):
        return pltpu.make_async_remote_copy(
            src_ref=q_ref.at[0, b, g],
            dst_ref=q_ref.at[1, b, g],
            send_sem=lend_sems.at[0, b, g],
            recv_sem=lend_sems.at[1, b, g],
            device_id={"group": lower},
            device_id_type=MESH,
        )

    per_group = tiles // kv_heads
    per_tile = wide // HD

    def head_group(g, carry):
        def tile(t, carry):
            index = g * per_group + t
            pltpu.make_async_copy(wq.at[index], wq.at[index], w_sems.at[index]).wait()
            product = jnp.dot(flat[...], wq[index], preferred_element_type=jnp.float32)
            for i in range(per_tile):
                turned[t * per_tile + i] = rotate(product[:, i * HD : (i + 1) * HD])
            return carry

        lax.fori_loop(0, per_group, tile, 0)
        for b in range(size):
            block = jnp.concatenate(
                [turned[h, b * count : (b + 1) * count, :] for h in range(heads)], axis=0
            )
            q_ref[0, b, g] = jnp.transpose(block).astype(q_ref.dtype)
            lend(b, g).start()
        return carry

    lax.fori_loop(0, kv_heads, head_group, 0)
    fetches[tiles].wait()
    product = jnp.dot(flat[...], wk[...], preferred_element_type=jnp.float32)
    for g in range(kv_heads):
        new_ref[:, g * 2 * HD : g * 2 * HD + HD] = rotate(product[:, g * HD : (g + 1) * HD]).astype(
            new_ref.dtype
        )
    fetches[tiles + 1].wait()
    product = jnp.dot(flat[...], wv[...], preferred_element_type=jnp.float32)
    for g in range(kv_heads):
        new_ref[:, g * 2 * HD + HD : (g + 1) * 2 * HD] = product[:, g * HD : (g + 1) * HD].astype(
            new_ref.dtype
        )
    for p in range(pieces):
        hand(p).wait_send()
    for step in range(size - 1):
        for p in range(pieces):
            for direction in (1, -1):

                @pl.when(sends(direction, step))
                def _(direction=direction, step=step, p=p):
                    part(direction, step, p).wait_send()

    for g in range(kv_heads):
        for b in range(size):
            lend(b, g).wait()


def hand_count(count):
    return 16 if count % 16 == 0 else count


def gather_rows(source, prefix_len, hidden, gain, wq, wk, wv, tensors):
    _, count, width = hidden.shape
    kv_heads = wk.shape[1] // HD
    heads = wq.shape[1] // wk.shape[1]
    wide = 2 * HD if heads % 2 == 0 else HD
    tiles = wq.shape[1] // wide
    total = count * tensors
    pieces = count // hand_count(count)
    half = np.arange(HD // 2, dtype=np.float64) * 2.0 / HD
    frequency = np.float32(THETA**-half)
    frequency = jnp.asarray(np.concatenate([frequency, frequency])[None, :])
    dtype = hidden.dtype
    return pl.pallas_call(
        gather_kernel,
        out_shape=(
            jax.ShapeDtypeStruct((count, width), dtype),
            jax.ShapeDtypeStruct((2, tensors, kv_heads, HD, heads * count), dtype),
            jax.ShapeDtypeStruct((total, 2 * wk.shape[1]), dtype),
        ),
        in_specs=[SMEM, SMEM, VMEM, VMEM, ANY, ANY, ANY, ANY],
        out_specs=(VMEM, VMEM, VMEM),
        scratch_shapes=[
            pltpu.VMEM((count, width), dtype),
            pltpu.VMEM((count, width), dtype),
            pltpu.VMEM((total, width), dtype),
            pltpu.VMEM((tiles, width, wide), dtype),
            pltpu.VMEM(wk.shape, dtype),
            pltpu.VMEM(wv.shape, dtype),
            pltpu.VMEM((total, HD), jnp.float32),
            pltpu.VMEM((total, HD), jnp.float32),
            pltpu.VMEM((heads, total, HD), jnp.float32),
            pltpu.SemaphoreType.DMA,
            pltpu.SemaphoreType.DMA((tiles + 2,)),
            pltpu.SemaphoreType.DMA((2, pieces)),
            pltpu.SemaphoreType.DMA((2, tensors, pieces)),
            pltpu.SemaphoreType.DMA((2, tensors, pieces)),
            pltpu.SemaphoreType.DMA((2, tensors, kv_heads)),
        ],
        compiler_params=pltpu.CompilerParams(collective_id=0, has_side_effects=True),
        name="gather_rows",
    )(source, prefix_len, frequency, gain.reshape(1, -1), hidden, wq, wk, wv)


def attend_kernel(
    source_ref, len_ref, table_ref, q_ref, new_ref, pool_ref, own_ref, lent_ref, m_ref, l_ref, acc, buf, sems
):
    me, groups = lax.axis_index("group"), lax.axis_size("group")
    _, blocks, kv_heads, _, span = q_ref.shape
    count = new_ref.shape[0] // blocks
    chunk = buf.shape[1]
    pages = chunk // PAGE
    region = pool_ref.shape[0] // 2
    own = jnp.where(source_ref[me] == me, len_ref[me, 0], 0)
    lent = jnp.where(source_ref[(me + 1) % groups] == me, len_ref[me, 1], 0)
    own_chunks = (own + chunk - 1) // chunk
    total = own_chunks + (lent + chunk - 1) // chunk

    def place(index):
        side = jnp.where(index >= own_chunks, 1, 0)
        return side, index - side * own_chunks

    def start(index, slot):
        side, within = place(index)
        for i in range(pages):
            page = table_ref[side, within * pages + i] + side * region
            pltpu.make_async_copy(
                pool_ref.at[page], buf.at[slot, pl.ds(i * PAGE, PAGE)], sems.at[slot]
            ).start()

    def wait(slot):
        pltpu.make_async_copy(buf.at[slot], buf.at[slot], sems.at[slot]).wait()

    def absorb(side, load, keys_of, mask_of):
        def settle(g, b, fade, weights):
            acc[side, b, g] = acc[side, b, g] * fade + lax.dot_general(
                load(g * 2 * HD + HD, keys_of(b)),
                weights,
                (((0,), (0,)), ((), ())),
                preferred_element_type=jnp.float32,
            )

        tasks = [(g, b) for g in range(kv_heads) for b in range(blocks)]

        def score(task):
            g, b = task
            return jnp.dot(
                load(g * 2 * HD, keys_of(b)), q_ref[side, b, g], preferred_element_type=jnp.float32
            )

        ahead = score(tasks[0])
        pending = None
        for i, (g, b) in enumerate(tasks):
            scores = ahead
            if i + 1 < len(tasks):
                ahead = score(tasks[i + 1])
            if mask_of is not None:
                scores = jnp.where(mask_of(b, scores.shape), scores, -jnp.inf)
            row = g * blocks + b
            old = m_ref[side, row : row + 1, :]
            top = jnp.maximum(old, jnp.max(scores, axis=0, keepdims=True))
            fade = jnp.exp2((old - top) * EXP_SCALE)
            weights = jnp.exp2((scores - top) * EXP_SCALE)
            m_ref[side, row : row + 1, :] = top
            l_ref[side, row : row + 1, :] = l_ref[side, row : row + 1, :] * fade + jnp.sum(
                weights, axis=0, keepdims=True
            )
            weights = weights.astype(jnp.bfloat16)
            if pending is not None:
                settle(*pending)
            pending = (g, b, fade, weights)
        settle(*pending)

    @pl.when(total > 0)
    def _():
        start(0, 0)

    m_ref[...] = jnp.full_like(m_ref, -jnp.inf)
    l_ref[...] = jnp.zeros_like(l_ref)
    acc[...] = jnp.zeros_like(acc)
    absorb(
        0,
        lambda c, keys: new_ref[:keys, c : c + HD],
        lambda b: (b + 1) * count,
        lambda b, shape: lax.broadcasted_iota(jnp.int32, shape, 0)
        <= lax.broadcasted_iota(jnp.int32, shape, 1) % count + b * count,
    )

    def step(index, carry):
        slot = index % 2
        wait(slot)

        @pl.when(index + 1 < total)
        def _():
            start(index + 1, 1 - slot)

        side, within = place(index)
        left = jnp.where(side > 0, lent, own) - within * chunk

        def load(c, keys):
            return buf[slot, :, c : c + HD]

        @pl.when(left >= chunk)
        def _():
            absorb(side, load, lambda b: chunk, None)

        @pl.when(left < chunk)
        def _():
            absorb(
                side,
                load,
                lambda b: chunk,
                lambda b, shape: lax.broadcasted_iota(jnp.int32, shape, 0) < left,
            )

        return carry

    lax.fori_loop(0, total, step, 0)
    own_ref[...] = acc[0]
    sums = l_ref[1]
    inverse = jnp.where(sums > 0.0, 1.0 / jnp.where(sums > 0.0, sums, 1.0), 0.0)
    for g in range(kv_heads):
        for b in range(blocks):
            row = g * blocks + b
            lent_ref[b, g] = (acc[1, b, g] * inverse[row : row + 1, :]).astype(lent_ref.dtype)


def attend(source, prefix_len, table, q, new_kv, pool):
    _, blocks, kv_heads, _, span = q.shape
    stat = jax.ShapeDtypeStruct((2, kv_heads * blocks, span), jnp.float32)
    keys = table.shape[1] * PAGE
    return pl.pallas_call(
        attend_kernel,
        out_shape=(
            jax.ShapeDtypeStruct(q.shape[1:], jnp.float32),
            jax.ShapeDtypeStruct(q.shape[1:], q.dtype),
            stat,
            stat,
        ),
        in_specs=[SMEM, SMEM, SMEM, VMEM, VMEM, ANY],
        out_specs=(VMEM, VMEM, VMEM, VMEM),
        scratch_shapes=[
            pltpu.VMEM(q.shape, jnp.float32),
            pltpu.VMEM((2, min(CHUNK, keys), pool.shape[2]), q.dtype),
            pltpu.SemaphoreType.DMA((2,)),
        ],
        cost_estimate=pl.CostEstimate(
            flops=4 * keys * kv_heads * blocks * span * HD,
            transcendentals=keys * kv_heads * blocks * span,
            bytes_accessed=2 * keys * pool.shape[2],
        ),
        name="attend",
    )(source, prefix_len, table, q, new_kv, pool)


def project_kernel(
    owner_ref,
    own_ref,
    lent_ref,
    m_ref,
    l_ref,
    rows_ref,
    new_ref,
    w_hbm,
    out_ref,
    pool_ref,
    part,
    stats,
    mixed,
    weights,
    sums,
    inbox,
    staged,
    landed,
    w_sems,
    part_sems,
    stat_sems,
    send,
    recv,
    page_send,
    page_recv,
    page_own,
):
    group, groups = lax.axis_index("group"), lax.axis_size("group")
    me, size = lax.axis_index("tensor"), lax.axis_size("tensor")
    count, width = rows_ref.shape
    tiles = weights.shape[0]
    wide = weights.shape[2]
    blocks, kv_heads, _, span = own_ref.shape
    heads = span // count
    box = staged.shape[0] // groups
    cap = box // PAGE

    def fetch(i):
        return pltpu.make_async_copy(
            w_hbm.at[:, pl.ds(pl.multiple_of(i * wide, wide), wide)], weights.at[i], w_sems.at[i]
        )

    for i in range(tiles):
        fetch(i).start()
    greet(
        pltpu.get_barrier_semaphore(), [(group + k) % groups for k in range(1, groups)], me, size
    )

    order = []
    for k in range((size + 1) // 2):
        order += [size - 1 - k] + ([k] if k != size - 1 - k else [])

    def give(index):
        if index < 2:
            source, target, sems = (m_ref, l_ref)[index].at[1], stats.at[index], stat_sems.at[index]
        else:
            source, target, sems = lent_ref.at[index - 2], part.at[index - 2], part_sems.at[index - 2]
        return pltpu.make_async_remote_copy(
            src_ref=source,
            dst_ref=target,
            send_sem=sems.at[0],
            recv_sem=sems.at[1],
            device_id={"group": (group + 1) % groups},
            device_id_type=MESH,
        )

    for index in [0, 1] + [2 + b for b in order]:
        give(index).start()

    def hop(direction, chunk):
        lane = 0 if direction > 0 else 1
        return pltpu.make_async_remote_copy(
            src_ref=sums.at[chunk],
            dst_ref=inbox.at[lane, chunk],
            send_sem=send.at[chunk],
            recv_sem=recv.at[lane, chunk],
            device_id={"tensor": jnp.clip(me + direction, 0, size - 1)},
            device_id_type=MESH,
        )

    give(0).wait_recv()
    give(1).wait_recv()
    for order_at, chunk in enumerate(order):
        give(2 + chunk).wait_recv()
        for g in range(kv_heads):
            row = slice(g * blocks + chunk, g * blocks + chunk + 1)
            own_max, part_max, part_sum = m_ref[0, row, :], stats[0, row, :], stats[1, row, :]
            top = jnp.maximum(own_max, part_max)
            own_scale = jnp.exp2((own_max - top) * EXP_SCALE)
            part_scale = jnp.exp2((part_max - top) * EXP_SCALE) * part_sum
            inverse = 1.0 / (l_ref[0, row, :] * own_scale + part_scale)
            value = own_ref[chunk, g] * (own_scale * inverse) + part[chunk, g].astype(
                jnp.float32
            ) * (part_scale * inverse)
            value = jnp.transpose(value).astype(mixed.dtype)
            for h in range(heads):
                mixed[:, (g * heads + h) * HD : (g * heads + h + 1) * HD] = value[
                    h * count : (h + 1) * count, :
                ]

        def product(i, carry, first=order_at == 0, chunk=chunk):
            if first:
                fetch(i).wait()
            sums[chunk, :, pl.ds(pl.multiple_of(i * wide, wide), wide)] = jnp.dot(
                mixed[...], weights[i], preferred_element_type=jnp.float32
            ).astype(sums.dtype)
            return carry

        lax.fori_loop(0, tiles, product, 0)
        if chunk > 0:

            @pl.when(me == 0)
            def _(chunk=chunk):
                hop(1, chunk).start()

        if chunk < size - 1:

            @pl.when(me == size - 1)
            def _(chunk=chunk):
                hop(-1, chunk).start()

    page_count = owner_ref.shape[1]
    tokens = new_ref.shape[0]
    slots = groups * box

    def iota(shape, axis):
        return lax.broadcasted_iota(jnp.int32, shape, axis).astype(jnp.float32)

    square = (page_count, page_count)
    diagonal = iota(square, 0) == iota(square, 1)
    earlier = iota(square, 0) < iota(square, 1)

    def column_of(row):
        return jnp.sum(jnp.where(diagonal, row, 0.0), axis=1, keepdims=True)

    def ranked(h):
        row = owner_ref[pl.ds(h, 1), :].astype(jnp.float32)
        same = jnp.logical_and(column_of(row) == row, earlier)
        return row, jnp.sum(jnp.where(same, 1.0, 0.0), axis=0, keepdims=True)

    row, rank = ranked(group)
    wide_pages = (page_count, tokens)
    page_of = (lax.broadcasted_iota(jnp.int32, wide_pages, 1) >> PAGE_BITS).astype(jnp.float32)
    slot = jnp.sum(
        jnp.where(page_of == iota(wide_pages, 0), column_of(row * cap + rank), 0.0),
        axis=0,
        keepdims=True,
    )
    within = (lax.broadcasted_iota(jnp.int32, (1, tokens), 1) & (PAGE - 1)).astype(jnp.float32)
    choose = iota((slots, tokens), 0) == slot * PAGE + within
    staged[...] = jnp.dot(
        jnp.where(choose, 1.0, 0.0).astype(jnp.bfloat16),
        new_ref[...],
        preferred_element_type=jnp.float32,
    ).astype(staged.dtype)

    def pages(k):
        peer = (group + k) % groups
        return pltpu.make_async_remote_copy(
            src_ref=staged.at[pl.ds(pl.multiple_of(peer * box, box), box)],
            dst_ref=landed.at[pl.ds(pl.multiple_of(group * box, box), box)],
            send_sem=page_send.at[k],
            recv_sem=page_recv.at[k],
            device_id={"group": peer},
            device_id_type=MESH,
        )

    mine = pl.ds(pl.multiple_of(group * box, box), box)
    keep_own = pltpu.make_async_copy(staged.at[mine], landed.at[mine], page_own)
    keep_own.start()
    for k in range(1, groups):
        pages(k).start()

    def relay(direction, chunk):
        lane = 0 if direction > 0 else 1
        hop(direction, chunk).wait_recv()

        def add(i, carry):
            span = pl.ds(pl.multiple_of(i * wide, wide), wide)
            sums[chunk, :, span] = (
                sums[chunk, :, span].astype(jnp.float32)
                + inbox[lane, chunk, :, span].astype(jnp.float32)
            ).astype(sums.dtype)
            return carry

        lax.fori_loop(0, tiles, add, 0)
        hop(direction, chunk).start()

    def up(chunk):
        @pl.when(jnp.logical_and(me > 0, me < chunk))
        def _():
            relay(1, chunk)

    def down(chunk):
        @pl.when(jnp.logical_and(me < size - 1, me > chunk))
        def _():
            relay(-1, chunk)

    @pl.when(me < size // 2)
    def _():
        for k in range(size):
            up(size - 1 - k)
            down(k)

    @pl.when(me >= size // 2)
    def _():
        for k in range(size):
            down(k)
            up(size - 1 - k)

    def locate(h, keep):
        row, rank = ranked(h)
        return keep + jnp.where(
            row == group.astype(jnp.float32), rank + (h * cap).astype(jnp.float32), 0.0
        )

    keep = lax.fori_loop(0, groups, locate, jnp.zeros((1, page_count), jnp.float32))
    tall = (tokens, page_count)
    page_at = (lax.broadcasted_iota(jnp.int32, tall, 0) >> PAGE_BITS).astype(jnp.float32)
    keep = jnp.sum(jnp.where(page_at == iota(tall, 1), keep, 0.0), axis=1, keepdims=True)
    inner = (lax.broadcasted_iota(jnp.int32, (tokens, 1), 0) & (PAGE - 1)).astype(jnp.float32)
    choose = iota((tokens, slots), 1) == keep * PAGE + inner
    keep_own.wait()
    for k in range(1, groups):
        pages(k).wait()
    pool_ref[...] = jnp.dot(
        jnp.where(choose, 1.0, 0.0).astype(jnp.bfloat16),
        landed[...],
        preferred_element_type=jnp.float32,
    ).astype(pool_ref.dtype)

    @pl.when(me > 0)
    def _():
        hop(1, me).wait_recv()

    @pl.when(me == 0)
    def _():
        inbox[0, me] = jnp.zeros(inbox.shape[2:], inbox.dtype)

    @pl.when(me < size - 1)
    def _():
        hop(-1, me).wait_recv()

    @pl.when(me == size - 1)
    def _():
        inbox[1, me] = jnp.zeros(inbox.shape[2:], inbox.dtype)

    def finish(i, carry):
        span = pl.ds(pl.multiple_of(i * wide, wide), wide)
        branch = sums[me, :, span].astype(jnp.float32) + (
            inbox[0, me, :, span].astype(jnp.float32) + inbox[1, me, :, span].astype(jnp.float32)
        )
        out_ref[:, span] = (rows_ref[:, span].astype(jnp.float32) + branch).astype(out_ref.dtype)
        return carry

    lax.fori_loop(0, tiles, finish, 0)
    for index in range(2 + size):
        give(index).wait_send()
    for chunk in range(size):

        @pl.when(me < chunk)
        def _(chunk=chunk):
            hop(1, chunk).wait_send()

        @pl.when(me > chunk)
        def _(chunk=chunk):
            hop(-1, chunk).wait_send()


def project(owner, own, lent, top, sums, rows, new_kv, weights):
    count, width = rows.shape
    groups, page_count = owner.shape
    tensors = own.shape[0]
    wide = 512 if width % 512 == 0 else width
    tiles = width // wide
    spread_count = min(groups, page_count - page_count // 4)
    cap = (page_count + spread_count - 1) // spread_count
    box = pltpu.VMEM((groups * cap * PAGE, new_kv.shape[1]), new_kv.dtype)
    return pl.pallas_call(
        project_kernel,
        out_shape=(
            jax.ShapeDtypeStruct((count, width), rows.dtype),
            jax.ShapeDtypeStruct(new_kv.shape, new_kv.dtype),
        ),
        in_specs=[VMEM] * 7 + [ANY],
        out_specs=(VMEM, VMEM),
        scratch_shapes=[
            pltpu.VMEM(lent.shape, lent.dtype),
            pltpu.VMEM((2,) + top.shape[1:], jnp.float32),
            pltpu.VMEM((count, weights.shape[0]), rows.dtype),
            pltpu.VMEM((tiles, weights.shape[0], wide), weights.dtype),
            pltpu.VMEM((tensors, count, width), rows.dtype),
            pltpu.VMEM((2, tensors, count, width), rows.dtype),
            box,
            box,
            pltpu.SemaphoreType.DMA((tiles,)),
            pltpu.SemaphoreType.DMA((tensors, 2)),
            pltpu.SemaphoreType.DMA((2, 2)),
            pltpu.SemaphoreType.DMA((tensors,)),
            pltpu.SemaphoreType.DMA((2, tensors)),
            pltpu.SemaphoreType.DMA((groups,)),
            pltpu.SemaphoreType.DMA((groups,)),
            pltpu.SemaphoreType.DMA,
        ],
        compiler_params=pltpu.CompilerParams(collective_id=1, has_side_effects=True),
        name="project",
    )(owner, own, lent, top, sums, rows, new_kv, weights)


def local(
    hidden,
    norm_gain,
    w_query,
    w_key,
    w_value,
    w_output,
    prefix_pool,
    page_table,
    prefix_len,
    source,
    decode_owner,
):
    tensors = lax.axis_size("tensor")
    rows, q, new_kv = gather_rows(
        source, prefix_len, hidden[0], norm_gain, w_query, w_key, w_value, tensors
    )
    own, lent, top, sums = attend(source, prefix_len, page_table[0], q, new_kv, prefix_pool)
    layer_out, kv_pool = project(decode_owner, own, lent, top, sums, rows, new_kv, w_output)
    return layer_out, kv_pool.reshape(-1, PAGE, kv_pool.shape[1])


def solution(mesh):
    return jax.shard_map(
        local,
        mesh=mesh,
        in_specs=(
            P("group", None, "tensor", None),
            P(),
            P(None, "tensor"),
            P(None, "tensor"),
            P(None, "tensor"),
            P("tensor", None),
            P("group", None, "tensor"),
            P("group", None, None),
            P(),
            P(),
            P(),
        ),
        out_specs=(P(("group", "tensor"), None), P("group", None, "tensor")),
        check_vma=False,
    )
```
